128 devices in a mesh: blk: 128 (over x, z, y, core).
Axes of the slice: x: 4, y: 4, z: 4, core: 2. Of those that a mesh axis runs over, the one named last changes fastest.
Arguments:
- f_blocks: float32 [128, 9, 256, 256], P('blk'), may hold values from -6 to 6
- p_blocks: float32 [128, 9, 256, 256], P('blk'), may hold values from -0.125 to 0.125
- f_mask: int32 [128, 9], P('blk'), may hold values 0 or 1
- p_mask: int32 [128, 9], P('blk'), may hold values 0 or 1
Outputs:
- commutator: float32 [128, 9, 256, 256], P('blk')
- gradient: float32 [128, 9, 256, 256], P('blk')
The draws below stay inside these ranges and needn't reach their ends.
All inputs are finite; a program needn't handle non-finite values. No bound on the sum of `f_mask` or of `p_mask` on one device may be relied on, other than what follows from the above.
Results may differ from the reference program's by a relative error of at most 0.0001.
Values sent between devices are 32-bit elements; how exact they have to be, the bound alone decides.
No kernel may reach another device: no remote copies, remote signals or barrier semaphores. Data moves between devices by JAX's collectives and lax.ppermute only.
A program may use at most 128 MiB of HBM per device.

```python
import jax
import jax.numpy as jnp
from jax import lax

BS = 256
HALF = 4
BAND = 9
NBR = 128


def set_ends(result, key, least, top_value):
    spot = [jax.random.randint(jax.random.fold_in(key, axis), (), 0, length) for axis, length in enumerate(result.shape)]
    main_axis = result.shape.index(max(result.shape))
    neighbour = spot[:main_axis] + [(spot[main_axis] + 1) % result.shape[main_axis]] + spot[main_axis + 1:]
    return result.at[tuple(spot)].set(least).at[tuple(neighbour)].set(top_value)


def shard_levels(key, dims, split, smallest, top_value):
    def one(dim, parts):
        steps = jax.random.uniform(jax.random.fold_in(jax.random.fold_in(key, 6), dim), (parts,), jnp.float32, smallest / len(split), top_value / len(split))
        return jnp.repeat(jnp.exp(steps), dims[dim] // parts).reshape((-1,) + (1,) * (len(dims) - dim - 1))

    factor_of = one(*split[0])
    for cut in split[1:]:
        factor_of = factor_of * one(*cut)
    return factor_of


def normal_values(stream_key, dims, scale, reach, shards=(), held_as=jnp.bfloat16):
    result = jax.random.normal(stream_key, dims, jnp.float32) * scale
    if len(shards) > 0:
        result = shard_levels(stream_key, dims, shards, -0.22, 0.18) * result
    return jnp.clip(result, min=-reach, max=reach).astype(held_as)


def setup_inputs(seed: int = 0) -> dict:
    seeds = jax.random.split(jax.random.key(seed), 5)
    return {
        "f_blocks": normal_values(seeds[0], (NBR, BAND, BS, BS), 1.0, 6.0, ((0, 128),), jnp.float32),
        "p_blocks": normal_values(seeds[1], (NBR, BAND, BS, BS), (BS * BAND) ** -0.5, 0.125, ((0, 128),), jnp.float32),
        "f_mask": set_ends((jax.random.randint(seeds[2], (NBR, BAND), 0, 4) < 3).astype(jnp.int32), jax.random.fold_in(seeds[2], 1), 0, 1),
        "p_mask": set_ends((jax.random.randint(seeds[3], (NBR, BAND), 0, 4) < 3).astype(jnp.int32), jax.random.fold_in(seeds[3], 1), 0, 1),
    }


def block_product(left, right, offset_list):
    total = jnp.zeros((left.shape[0], BAND, BS, BS), jnp.float32)
    for o in range(-HALF, HALF + 1):
        acc = jnp.zeros((left.shape[0], BS, BS), jnp.float32)
        for a in range(-HALF, HALF + 1):
            if abs(o - a) <= HALF:
                moved = jnp.roll(right[:, o - a + HALF], -a, axis=0)
                acc = acc + jnp.einsum("rij,rjk->rik", left[:, a + HALF], moved, precision=lax.Precision.HIGHEST)
        total = total.at[:, o + HALF].set(acc)
    return total


def reference(f_blocks, p_blocks, f_mask, p_mask):
    fmat = f_blocks * f_mask[:, :, None, None].astype(jnp.float32)
    pmat = p_blocks * p_mask[:, :, None, None].astype(jnp.float32)
    xmat = block_product(fmat, pmat, None)
    commutator = jnp.zeros_like(xmat)
    for o in range(-HALF, HALF + 1):
        mirrored = jnp.roll(xmat[:, -o + HALF], -o, axis=0)
        commutator = commutator.at[:, o + HALF].set(xmat[:, o + HALF] - jnp.swapaxes(mirrored, -1, -2))
    gradient = block_product(commutator, pmat, None)
    return commutator, gradient
```

```python
import jax
import jax.numpy as jnp
from jax import lax
from jax.experimental import pallas as pl
from jax.experimental.pallas import tpu as pltpu
from jax.sharding import PartitionSpec as P

BF = jnp.bfloat16
F32 = jnp.float32
ANY = pl.BlockSpec(memory_space=pl.ANY)
SMEM = pl.BlockSpec(memory_space=pltpu.SMEM)


def place(odd, k):
    return k + odd * (8 - 2 * k)


def send(value, offset):
    n = lax.axis_size("blk")
    return lax.ppermute(value, "blk", [(d, (d + offset if d % 2 == 0 else d - offset) % n) for d in range(n)])


def split(x):
    hi = x.astype(BF)
    return hi, (x - hi.astype(F32)).astype(BF)


def dot3(lhi, llo, rhi, rlo):
    dot = lambda a, b: jnp.dot(a, b, preferred_element_type=F32)
    return dot(lhi, rhi) + (dot(llo, rhi) + dot(lhi, rlo))


def mask_kernel(odd_ref, mask_ref, p_ref, out_ref, buf, isem, osem):
    odd = odd_ref[0]
    ins = [pltpu.make_async_copy(p_ref.at[0, place(odd, k)], buf.at[k], isem.at[k]) for k in range(9)]
    outs = [pltpu.make_async_copy(buf.at[k], out_ref.at[k], osem.at[k]) for k in range(9)]
    for c in ins:
        c.start()
    for k in range(9):
        ins[k].wait()
        buf[k] = buf[k] * mask_ref[0, place(odd, k)].astype(F32)
        outs[k].start()
    for c in outs:
        c.wait()


def masked(odd, mask, p):
    bs = p.shape[-1]
    return pl.pallas_call(
        mask_kernel,
        in_specs=[SMEM, SMEM, ANY],
        out_specs=ANY,
        out_shape=jax.ShapeDtypeStruct((9, bs, bs), F32),
        scratch_shapes=[pltpu.VMEM((9, bs, bs), F32), pltpu.SemaphoreType.DMA((9,)), pltpu.SemaphoreType.DMA((9,))],
        cost_estimate=pl.CostEstimate(flops=0, bytes_accessed=18 * bs * bs * 4, transcendentals=0),
        name="mask_p",
    )(odd, mask, p)


def run_terms(terms, sources, src_refs, pbuf, psem, lhs_of, out_of, table_ref, lhi, llo, acc):
    def step(i, carry):
        pltpu.make_async_copy(pbuf.at[i], pbuf.at[i], psem.at[i]).wait()
        rhi, rlo = split(pbuf[i])
        a = table_ref[0, i]
        o = table_ref[1, i]
        acc[o] = acc[o] + dot3(lhi[a], llo[a], rhi, rlo)
        return carry

    lax.fori_loop(0, len(terms), step, 0)


def product(name, odd, f, mask, terms, sources, outs, base=None, base_at=None, groups=None):
    bs = f.shape[-1]
    lhs = sorted({t[2] for t in terms})
    table = jnp.array([[lhs.index(t[2]) for t in terms], [outs.index(t[3]) for t in terms]], jnp.int32)
    groups = groups or [outs]
    nl, nt, no = len(lhs), len(terms), len(outs)
    names = list(sources)
    ng = len(groups)

    def kernel(odd_ref, mask_ref, table_ref, f_ref, *refs):
        refs = list(refs)
        base_ref = refs.pop(0) if base is not None else None
        src = dict(zip(names, refs[: len(names)]))
        out_refs = refs[len(names) : len(names) + ng]
        lraw, lhi, llo, pbuf, acc, lsem, psem, bsem, osem = refs[len(names) + ng :]
        odd = odd_ref[0]
        lcopies = [pltpu.make_async_copy(f_ref.at[0, place(odd, a + 4)], lraw.at[i], lsem.at[i]) for i, a in enumerate(lhs)]
        for c in lcopies:
            c.start()
        bcopies = []
        if base is not None:
            bcopies = [pltpu.make_async_copy(base_ref.at[base_at(o)], acc.at[i], bsem.at[i]) for i, o in enumerate(outs)]
            for c in bcopies:
                c.start()
        for i, t in enumerate(terms):
            pltpu.make_async_copy(src[t[0]].at[t[1]], pbuf.at[i], psem.at[i]).start()
        for i, a in enumerate(lhs):
            lcopies[i].wait()
            hi, lo = split(lraw[i] * mask_ref[0, place(odd, a + 4)].astype(F32))
            lhi[i] = hi
            llo[i] = lo
        if base is None:
            acc[...] = jnp.zeros_like(acc)
        for c in bcopies:
            c.wait()
        run_terms(terms, names, src, pbuf, psem, None, None, table_ref, lhi, llo, acc)
        ocopies = []
        for g, group in enumerate(groups):
            for j, o in enumerate(group):
                i = outs.index(o)
                ocopies.append(pltpu.make_async_copy(acc.at[i], out_refs[g].at[j], osem.at[i]))
                ocopies[-1].start()
        for c in ocopies:
            c.wait()

    args = [odd, mask, table, f] + ([base] if base is not None else []) + [sources[n] for n in names]
    return pl.pallas_call(
        kernel,
        in_specs=[SMEM, SMEM, SMEM] + [ANY] * (len(args) - 3),
        out_specs=[ANY] * ng,
        out_shape=[jax.ShapeDtypeStruct((len(g), bs, bs), F32) for g in groups],
        scratch_shapes=[
            pltpu.VMEM((nl, bs, bs), F32),
            pltpu.VMEM((nl, bs, bs), BF),
            pltpu.VMEM((nl, bs, bs), BF),
            pltpu.VMEM((nt, bs, bs), F32),
            pltpu.VMEM((no, bs, bs), F32),
            pltpu.SemaphoreType.DMA((nl,)),
            pltpu.SemaphoreType.DMA((nt,)),
            pltpu.SemaphoreType.DMA((no,)),
            pltpu.SemaphoreType.DMA((no,)),
        ],
        compiler_params=pltpu.CompilerParams(vmem_limit_bytes=56 * 1024 * 1024),
        cost_estimate=pl.CostEstimate(flops=6 * nt * bs**3, bytes_accessed=(nt + 2 * no + nl) * bs * bs * 4, transcendentals=0),
        name=name,
    )(*args)


def gradient(name, odd, own, mirror, terms, sources, cbuf=None, base=None, last=False):
    lhs = list(own)
    bs = sources[next(iter(sources))].shape[-1]
    outs = list(range(-4, 5))
    table = jnp.array([[lhs.index(t[2]) for t in terms], [outs.index(t[3]) for t in terms]], jnp.int32)
    nl, nt, no = len(lhs), len(terms), 9
    names = list(sources)
    arrays = []
    for a in lhs:
        for v in (own[a][0], mirror[a][0]):
            if not any(v is w for w in arrays):
                arrays.append(v)
    pick = lambda v: next(i for i, w in enumerate(arrays) if w is v)

    def kernel(odd_ref, table_ref, *refs):
        refs = list(refs)
        if cbuf is not None:
            refs.pop(0)
        base_ref = refs.pop(0) if base is not None else None
        arr = refs[: len(arrays)]
        refs = refs[len(arrays) :]
        src = dict(zip(names, refs[: len(names)]))
        c_ref, g_ref = refs[len(names) : len(names) + 2]
        xbuf, mbuf, lhi, llo, pbuf, acc, xsem, msem, csem, psem, bsem, osem = refs[len(names) + 2 :]
        odd = odd_ref[0]
        xc = [pltpu.make_async_copy(arr[pick(own[a][0])].at[own[a][1]], xbuf.at[i], xsem.at[i]) for i, a in enumerate(lhs)]
        mc = [pltpu.make_async_copy(arr[pick(mirror[a][0])].at[mirror[a][1]], mbuf.at[i], msem.at[i]) for i, a in enumerate(lhs)]
        for i in range(nl):
            xc[i].start()
            mc[i].start()
        bcopies = []
        if base is not None:
            bcopies = [pltpu.make_async_copy(base_ref.at[i], acc.at[i], bsem.at[i]) for i in range(no)]
            for c in bcopies:
                c.start()
        for i, t in enumerate(terms):
            pltpu.make_async_copy(src[t[0]].at[t[1]], pbuf.at[i], psem.at[i]).start()
        cc = [pltpu.make_async_copy(xbuf.at[i], c_ref.at[0, place(odd, a + 4)], csem.at[i]) for i, a in enumerate(lhs)]
        for i in range(nl):
            xc[i].wait()
            mc[i].wait()
            c = xbuf[i] - mbuf[i].T
            xbuf[i] = c
            hi, lo = split(c)
            lhi[i] = hi
            llo[i] = lo
            cc[i].start()
        if base is None:
            acc[...] = jnp.zeros_like(acc)
        for c in bcopies:
            c.wait()
        run_terms(terms, names, src, pbuf, psem, None, None, table_ref, lhi, llo, acc)
        gc = []
        for i in range(no):
            dst = g_ref.at[0, place(odd, i)] if last else g_ref.at[i]
            gc.append(pltpu.make_async_copy(acc.at[i], dst, osem.at[i]))
            gc[-1].start()
        for c in cc + gc:
            c.wait()

    args = [odd, table] + ([cbuf] if cbuf is not None else []) + ([base] if base is not None else []) + arrays + [sources[n] for n in names]
    gshape = (1, 9, bs, bs) if last else (9, bs, bs)
    return pl.pallas_call(
        kernel,
        in_specs=[SMEM, SMEM] + [ANY] * (len(args) - 2),
        out_specs=[ANY, ANY],
        out_shape=[jax.ShapeDtypeStruct((1, 9, bs, bs), F32), jax.ShapeDtypeStruct(gshape, F32)],
        scratch_shapes=[
            pltpu.VMEM((nl, bs, bs), F32),
            pltpu.VMEM((nl, bs, bs), F32),
            pltpu.VMEM((nl, bs, bs), BF),
            pltpu.VMEM((nl, bs, bs), BF),
            pltpu.VMEM((nt, bs, bs), F32),
            pltpu.VMEM((no, bs, bs), F32),
            pltpu.SemaphoreType.DMA((nl,)),
            pltpu.SemaphoreType.DMA((nl,)),
            pltpu.SemaphoreType.DMA((nl,)),
            pltpu.SemaphoreType.DMA((nt,)),
            pltpu.SemaphoreType.DMA((no,)),
            pltpu.SemaphoreType.DMA((no,)),
        ],
        input_output_aliases={2: 0} if cbuf is not None else {},
        compiler_params=pltpu.CompilerParams(vmem_limit_bytes=56 * 1024 * 1024),
        cost_estimate=pl.CostEstimate(flops=6 * nt * bs**3, bytes_accessed=(nt + 2 * no + 3 * nl) * bs * bs * 4, transcendentals=0),
        name=name,
    )(*args)


def terms_of(a, first, last, source, block):
    return [(source, block(s), a, a + s) for s in range(first, last + 1)]


def body(f, p, f_mask, p_mask):
    odd = (lax.axis_index("blk") % 2).astype(jnp.int32).reshape(1)
    pm = masked(odd, p_mask, p)
    t1 = send(pm[2:9], 2)
    q0 = send(pm, 1)
    t2 = send(q0[0:8], 2)
    qt1 = send(t1, 1)
    b1 = send(t1[2:7], 2)
    qt2 = send(t2, 1)
    b2a = send(t2[2:6], 2)
    b2b = send(t2[0:2], 2)
    qb2a = send(b2a, 1)
    qb2b = send(b2b, 1)
    src = dict(pm=pm, q0=q0, t1=t1, t2=t2, b1=b1, b2a=b2a, b2b=b2b, qt1=qt1, qt2=qt2, qb2a=qb2a, qb2b=qb2b)
    rows = {
        0: terms_of(0, -4, 4, "pm", lambda s: s + 4),
        1: terms_of(1, -4, 3, "q0", lambda s: 4 - s),
        -2: terms_of(-2, -2, 4, "t1", lambda s: s + 2),
        -1: terms_of(-1, -3, 4, "t2", lambda s: 4 - s),
        3: terms_of(3, -4, 1, "qt1", lambda s: 2 - s),
        2: terms_of(2, -4, 2, "qt2", lambda s: s + 4),
        -4: terms_of(-4, 0, 4, "b1", lambda s: s),
        -3: terms_of(-3, -1, 2, "b2a", lambda s: 2 - s) + terms_of(-3, 3, 4, "b2b", lambda s: 4 - s),
        4: terms_of(4, -4, -3, "qb2b", lambda s: s + 4) + terms_of(4, -2, 0, "qb2a", lambda s: s + 2),
    }
    use = lambda terms: {n: src[n] for n in dict.fromkeys(t[0] for t in terms)}
    every = list(range(-4, 5))
    near = rows[0] + rows[1] + rows[-2] + rows[3] + rows[-1] + rows[2]
    (part,) = product("x_near", odd, f, f_mask, near, use(near), every)
    far = rows[-4] + rows[-3] + rows[4]
    x = {}
    for name, outs in (("x_down", [-4, -3, -2, -1]), ("x_up", [4, 3, 2]), ("x_mid", [0, 1])):
        terms = [t for t in far if t[3] in outs]
        found = product(name, odd, f, f_mask, terms, use(terms), outs, part, lambda o: o + 4, [[o] for o in outs])
        x.update(zip(outs, found))
    mirror = {0: x[0]}
    for o in (-4, -3, 4, -2, -1, 3, 2, 1):
        mirror[o if o % 2 else -o] = send(x[o], o)
    early = (0, 1, -4, 4, -3)
    late = (-1, -2, 2, 3)
    pair = lambda d, offsets: {a: (d[a], 0) for a in offsets}
    terms = [t for a in early for t in rows[a]]
    com, part_g = gradient("g_early", odd, pair(x, early), pair(mirror, early), terms, use(terms))
    terms = [t for a in late for t in rows[a]]
    com, grad = gradient("g_late", odd, pair(x, late), pair(mirror, late), terms, use(terms), com, part_g, True)
    return com, grad


def solution(mesh):
    in_specs = (
        P("blk", None, None, None),
        P("blk", None, None, None),
        P("blk", None),
        P("blk", None),
    )
    out_specs = (P("blk", None, None, None), P("blk", None, None, None))
    return jax.shard_map(body, mesh=mesh, in_specs=in_specs, out_specs=out_specs, check_vma=False)
```
